768 devices in a mesh: gx: 12 (over z), gy: 16 (over y, core), band: 4 (over x).
Axes of the slice: x: 4, y: 8, z: 12, core: 2. Of those that a mesh axis runs over, the one named last changes fastest.
Arguments:
- orbitals: float32 [8, 384, 128, 256], P('band', 'gx', 'gy'), may hold values from -600 to 600
- potential: float32 [384, 128, 256], P('gx', 'gy'), may hold values from -0.5 to 0.5
- order: int32 [8], replicated, may hold values from 0 to 7, as said below
Outputs:
- basis: float32 [8, 384, 128, 256], P('band', 'gx', 'gy')
The draws below stay inside these ranges and needn't reach their ends.
Inputs may be any that keep to these rules, and one draw needn't show every extreme that they name: `order`: each orbital appears once; position p names the orbital orthonormalized p-th.
All inputs are finite; a program needn't handle non-finite values.
Results may differ from the reference program's by a relative error of at most 0.00026.
Values sent between devices are 32-bit elements; how exact they have to be, the bound alone decides.
A program may use at most 32 MiB of HBM per device.

```python
import jax
import jax.numpy as jnp
from jax import lax

NZ = 256
DEGREE = 8
NX = 384
NY = 128
ORBS = 8


def draw_orbitals(key, part):
    keys = jax.random.split(key, 3)
    along_x = jnp.arange(NX, dtype=jnp.float32) / max(NX - 1, 1)
    along_y = jnp.arange(NY, dtype=jnp.float32) / max(NY - 1, 1)
    cell_scale = 10.0 ** (0.5 * (along_x[:, None] + along_y[None, :]))
    orbital_scale = 10.0 ** jax.random.uniform(keys[1], (ORBS,), jnp.float32)
    noise = jax.random.normal(keys[0], (ORBS, NX, NY, NZ), jnp.float32)
    shared = jax.random.normal(keys[2], (1, NX, NY, NZ), jnp.float32)
    values = jnp.clip(0.8 * noise + 0.6 * shared, -6.0, 6.0)
    return values * orbital_scale[:, None, None, None] * cell_scale[None, :, :, None]


def draw_order(key, part):
    return jax.random.permutation(jax.random.fold_in(key, 17), jnp.arange(ORBS, dtype=jnp.int32)).astype(jnp.int32)


def steps_of(own_key, dims, shards, smallest, high):
    def one(dim, blocks):
        draws = jax.random.uniform(jax.random.fold_in(jax.random.fold_in(own_key, 6), dim), (blocks,), jnp.float32, smallest / len(shards), high / len(shards))
        return jnp.repeat(jnp.exp(draws), dims[dim] // blocks).reshape((-1,) + (1,) * (len(dims) - dim - 1))

    level = one(*shards[0])
    for cut in shards[1:]:
        level = level * one(*cut)
    return level


def setup_inputs(seed: int = 0) -> dict:
    key_list = jax.random.split(jax.random.key(seed), 4)
    orbitals = draw_orbitals(jax.random.fold_in(key_list[3], 71), 0)
    potential = jnp.clip(jax.random.uniform(key_list[1], (NX, NY, NZ), jnp.float32, -0.5, 0.5) * steps_of(key_list[1], (NX, NY, NZ), ((0, 12), (1, 16)), -0.4, 0.0), -0.5, 0.5)
    order = draw_order(jax.random.fold_in(key_list[3], 71), 0)
    return {"orbitals": orbitals, "potential": potential, "order": order}


def apply_operator(extended, potential):
    middle = extended[:, 2:-2, 2:-2, :]
    padded_z = jnp.pad(middle, ((0, 0), (0, 0), (0, 0), (2, 2)))
    nearest = extended[:, 1:-3, 2:-2] + extended[:, 3:-1, 2:-2]
    nearest = nearest + extended[:, 2:-2, 1:-3] + extended[:, 2:-2, 3:-1]
    nearest = nearest + padded_z[..., 1:-3] + padded_z[..., 3:-1]
    distant = extended[:, :-4, 2:-2] + extended[:, 4:, 2:-2]
    distant = distant + extended[:, 2:-2, :-4] + extended[:, 2:-2, 4:]
    distant = distant + padded_z[..., :-4] + padded_z[..., 4:]
    applied = (3.75 + potential) * middle - nearest * (2.0 / 3.0) + distant / 24.0
    return (applied - 4.25 * middle) / 4.25

def widen(field):
    return jnp.pad(field, ((0, 0), (2, 2), (2, 2), (0, 0)))

def filter_one(field, potential):
    previous = field[None]
    current = apply_operator(widen(previous), potential)
    for repeat in range(DEGREE - 1):
        following = 2.0 * apply_operator(widen(current), potential) - previous
        previous, current = (current, following)
    return current[0]

def mixing_matrix(correlation, order):
    orbital_count = correlation.shape[0]
    positions = jnp.arange(orbital_count, dtype=jnp.int32)
    target = order.astype(jnp.int32)
    arrange = (target[:, None] == positions[None, :]).astype(jnp.float32)
    highest = lax.Precision.HIGHEST
    ordered = jnp.dot(jnp.dot(arrange, correlation, precision=highest), arrange.T, precision=highest)
    lower_factor = jnp.linalg.cholesky(ordered)
    inverse = jax.scipy.linalg.solve_triangular(lower_factor, jnp.eye(orbital_count, dtype=jnp.float32), lower=True)
    return jnp.dot(jnp.dot(arrange.T, inverse, precision=highest), arrange, precision=highest)

def reference(orbitals, potential, order):
    filtered = lax.map(lambda field: filter_one(field, potential), orbitals)
    flattened = filtered.reshape(ORBS, -1)
    correlation = jnp.dot(flattened.astype(jnp.float32), flattened.T.astype(jnp.float32), precision=lax.Precision.HIGHEST, preferred_element_type=jnp.float32) / float(NX * NY * NZ)
    mixing = mixing_matrix(correlation, order)
    basis = jnp.dot(mixing.astype(jnp.float32), flattened.astype(jnp.float32), precision=lax.Precision.HIGHEST, preferred_element_type=jnp.float32)
    return basis.reshape(orbitals.shape)
```

```python
import functools

import jax
import jax.numpy as jnp
from jax import lax
from jax.experimental import pallas as pl
from jax.experimental.pallas import tpu as pltpu
from jax.sharding import PartitionSpec as P

DEGREE = 8
MESH = pl.DeviceIdType.MESH
F32 = jnp.float32
FAR = 2.0 / (24.0 * 4.25)

NXL, NYL = 32, 8
X0, XROWS, Y0, YROWS = 8, 48, 2, 12


def kernel(sizes, orb_ref, pot_ref, order_ref, out_ref, u, g, pp, v, w, s1, s2, s3, r1, r2, r3,
           hs, hr, as_, ar, bs, br, rs, rr):
    n_gx, n_gy, n_band = sizes
    gx, gy, band = lax.axis_index("gx"), lax.axis_index("gy"), lax.axis_index("band")
    names = (("band", band, n_band), ("gy", gy, n_gy), ("gx", gx, n_gx))

    zero_y = jnp.zeros((2, 2, 2, 2, 32, 128), F32)
    zero_x = jnp.zeros((2, 2, YROWS, 2, 2, 128), F32)

    @pl.when(gy == 0)
    def _():
        u[:, :, 0:2, :, X0:X0 + NXL, :] = zero_y

    @pl.when(gy == n_gy - 1)
    def _():
        u[:, :, 10:12, :, X0:X0 + NXL, :] = zero_y

    @pl.when(gx == 0)
    def _():
        u[:, :, :, :, 6:8, :] = zero_x

    @pl.when(gx == n_gx - 1)
    def _():
        u[:, :, :, :, 40:42, :] = zero_x

    barrier = pltpu.get_barrier_semaphore()
    for name, me, count in names:
        def greet(d, c, name=name, me=me, count=count):
            pl.semaphore_signal(barrier, inc=1, device_id={name: lax.rem(me + d, count)}, device_id_type=MESH)
            return c
        lax.fori_loop(1, count, greet, 0)

    def bring(x, c):
        for zt in range(2):
            for o in range(2):
                v[o, pl.ds(zt * NXL + x, NYL, stride=2 * NXL), :] = orb_ref[o, x, :, zt * 128:zt * 128 + 128]
            w[pl.ds(zt * NXL + x, NYL, stride=2 * NXL), :] = pot_ref[x, :, zt * 128:zt * 128 + 128]
        return c

    lax.fori_loop(0, NXL, bring, 0)

    def place(y, c):
        for zt in range(2):
            for xt in range(4):
                rows_in = pl.ds(y * 64 + zt * NXL + 8 * xt, 8)
                for o in range(2):
                    u[o, 0, Y0 + y, zt, pl.ds(X0 + 8 * xt, 8), :] = v[o, rows_in, :]
                pp[y, zt, pl.ds(8 * xt, 8), :] = (w[rows_in, :] - 0.5) * (2.0 / 4.25)
        return c

    lax.fori_loop(0, NYL, place, 0)
    pl.semaphore_wait(barrier, n_band + n_gy + n_gx - 3)

    sends_ok = (gy > 0, gy < n_gy - 1, gx > 0, gx < n_gx - 1)
    recvs_ok = (gy < n_gy - 1, gy > 0, gx < n_gx - 1, gx > 0)
    ids = ({"gy": gy - 1}, {"gy": gy + 1}, {"gx": gx - 1}, {"gx": gx + 1})
    xs = pl.ds(X0, NXL)
    ys = pl.ds(Y0, NYL)
    spans = (
        ((pl.ds(2, 2), xs), (pl.ds(10, 2), xs)),
        ((pl.ds(8, 2), xs), (pl.ds(0, 2), xs)),
        ((ys, pl.ds(8, 2)), (ys, pl.ds(40, 2))),
        ((ys, pl.ds(38, 2)), (ys, pl.ds(6, 2))),
    )

    def halo(o, p, way):
        (sy, sx), (dy, dx) = spans[way]
        return pltpu.make_async_remote_copy(
            src_ref=u.at[o, p, sy, :, sx, :], dst_ref=u.at[o, p, dy, :, dx, :],
            send_sem=hs.at[o, p, way], recv_sem=hr.at[o, p, way],
            device_id=ids[way], device_id_type=MESH)

    def send(o, p, ways):
        for way in ways:
            @pl.when(sends_ok[way])
            def _(way=way):
                halo(o, p, way).start()

    def arrive(o, p):
        for way in range(4):
            @pl.when(recvs_ok[way])
            def _(way=way):
                halo(o, p, way).wait_recv()

            @pl.when(sends_ok[way])
            def _(way=way):
                halo(o, p, way).wait_send()

    lane = lax.broadcasted_iota(jnp.int32, (8, 128), 1)
    sub = lax.broadcasted_iota(jnp.int32, (8, 128), 0)

    def rows(o, k, lo, hi):
        p = k % 2
        cur, prev = u.at[o, p], u.at[o, 1 - p]

        def body(y, c):
            yy = y + Y0
            for xt in range(4):
                r = X0 + 8 * xt
                mid = [cur[yy, zt, pl.ds(r, 8), :] for zt in range(2)]
                none = jnp.zeros_like(mid[0])
                for zt in range(2):
                    m = mid[zt]
                    after = mid[1] if zt == 0 else none
                    before = mid[0] if zt == 1 else none
                    near = cur[yy, zt, pl.ds(r - 1, 8), :] + cur[yy, zt, pl.ds(r + 1, 8), :]
                    near = near + (cur[yy - 1, zt, pl.ds(r, 8), :] + cur[yy + 1, zt, pl.ds(r, 8), :])
                    near = near + (pltpu.roll(jnp.where(lane < 1, after, m), 127, 1)
                                   + pltpu.roll(jnp.where(lane >= 127, before, m), 1, 1))
                    far = cur[yy, zt, pl.ds(r - 2, 8), :] + cur[yy, zt, pl.ds(r + 2, 8), :]
                    far = far + (cur[yy - 2, zt, pl.ds(r, 8), :] + cur[yy + 2, zt, pl.ds(r, 8), :])
                    far = far + (pltpu.roll(jnp.where(lane < 2, after, m), 126, 1)
                                 + pltpu.roll(jnp.where(lane >= 126, before, m), 2, 1))
                    value = pp[y, zt, pl.ds(8 * xt, 8), :] * m + (far - 16.0 * near) * FAR
                    if k == 0:
                        value = value * 0.5
                    else:
                        value = value - prev[yy, zt, pl.ds(r, 8), :]
                    if k == DEGREE - 1:
                        g[o, band, y, zt, pl.ds(8 * xt, 8), :] = value
                    else:
                        prev[yy, zt, pl.ds(r, 8), :] = value
            return c

        lax.fori_loop(lo, hi, body, 0)

    def quarter(o, d, turn):
        peer = lax.rem(band + d, n_band)
        part = lax.rem(peer + turn, n_band)
        block = g.at[o, band, pl.ds(2 * part, 2)]
        sem = (as_.at[o], ar.at[o]) if turn == 0 else (bs.at[o], br.at[o])
        return pltpu.make_async_remote_copy(
            src_ref=block, dst_ref=block, send_sem=sem[0], recv_sem=sem[1],
            device_id={"band": peer}, device_id_type=MESH)

    for o in range(2):
        send(o, 0, range(4))
    for k in range(DEGREE):
        for o in range(2):
            arrive(o, k % 2)
            last = k == DEGREE - 1
            rows(o, k, 0, 2)
            if not last:
                send(o, 1 - k % 2, (0,))
            rows(o, k, 6, 8)
            if not last:
                send(o, 1 - k % 2, (1,))
            rows(o, k, 2, 6)
            if not last:
                send(o, 1 - k % 2, (2, 3))
            else:
                for d in range(1, n_band):
                    quarter(o, d, 0).start()

    def both(o, first, count, sems):
        block = g.at[o, pl.ds(0, first), pl.ds(0, count)]
        pltpu.make_async_copy(block, block, sems[1].at[o]).wait()
        pltpu.make_async_copy(block, block, sems[0].at[o]).wait()

    for o in range(2):
        both(o, n_band - 1, 2, (as_, ar))

    orbs = 2 * n_band
    pairs = [(i, j) for i in range(orbs) for j in range(i + 1)]

    def correlate(t, sums):
        y, zt = 2 * band + t // 2, t % 2
        sums = list(sums)
        for xt in range(4):
            f = [g[i % 2, i // 2, y, zt, pl.ds(8 * xt, 8), :] for i in range(orbs)]
            sums = [a + f[i] * f[j] for a, (i, j) in zip(sums, pairs)]
        return tuple(sums)

    sums = lax.fori_loop(0, 4, correlate, tuple(jnp.zeros((8, 128), F32) for _ in pairs))
    flat = {}
    for a, (i, j) in zip(sums, pairs):
        flat[i, j] = flat[j, i] = jnp.sum(a, axis=0, keepdims=True)
    corr = jnp.zeros((8, 128), F32)
    for j in range(orbs):
        column = jnp.sum(jnp.concatenate([flat[i, j] for i in range(orbs)], axis=0), axis=1, keepdims=True)
        corr = jnp.where(lane == j, column, corr)

    for index, ((name, me, count), src, dst) in enumerate(zip(names, (s1, s2, s3), (r1, r2, r3))):
        src[...] = corr

        def give(d, c, name=name, me=me, count=count, src=src, dst=dst, index=index):
            pltpu.make_async_remote_copy(
                src_ref=src, dst_ref=dst.at[d - 1], send_sem=rs.at[index], recv_sem=rr.at[index],
                device_id={name: lax.rem(me + d, count)}, device_id_type=MESH).start()
            return c

        lax.fori_loop(1, count, give, 0)
        if index == 0:
            for turn in range(1, n_band):
                for o in range(2):
                    for d in range(1, n_band):
                        quarter(o, d, turn).start()
        pltpu.make_async_copy(dst, dst, rr.at[index]).wait()
        for d in range(count - 1):
            corr = corr + dst[d]
    cells = float(n_gx * NXL * n_gy * NYL * 256)
    state = jnp.where(lane < 8, corr * (1.0 / cells), jnp.where(lane == sub + 8, 1.0, 0.0))
    waiting = jnp.ones((8, 128), F32)
    pivots = jnp.ones((8, 128), F32)
    for position in range(orbs):
        j = order_ref[position]
        row = jnp.sum(jnp.where(sub == j, state, 0.0), axis=0, keepdims=True)
        column = jnp.sum(jnp.where(lane == j, state, 0.0), axis=1, keepdims=True)
        pivot = jnp.sum(jnp.where(lane[0:1] == j, row, 0.0), axis=1, keepdims=True)
        waiting = jnp.where(sub == j, 0.0, waiting)
        state = state - (waiting * (column / pivot)) * row
        pivots = jnp.where(sub == j, pivot, pivots)
    mixing = state / jnp.sqrt(pivots)

    weights = []
    for o in range(2):
        own = jnp.sum(jnp.where(sub == 2 * band + o, mixing, 0.0), axis=0, keepdims=True)
        weights.append([jnp.broadcast_to(jnp.sum(jnp.where(lane[0:1] == 8 + j, own, 0.0), axis=1, keepdims=True), (8, 128))
                        for j in range(orbs)])

    for o in range(2):
        both(o, n_band - 1, 6, (bs, br))
    for index, dst in enumerate((r1, r2, r3)):
        pltpu.make_async_copy(dst, dst, rs.at[index]).wait()

    def combine(y, c):
        for zt in range(2):
            for xt in range(4):
                f = [g[i % 2, i // 2, y, zt, pl.ds(8 * xt, 8), :] for i in range(orbs)]
                for o in range(2):
                    total = weights[o][0] * f[0]
                    for i in range(1, orbs):
                        total = total + weights[o][i] * f[i]
                    v[o, pl.ds(y * 64 + zt * 32 + 8 * xt, 8), :] = total
        return c

    lax.fori_loop(0, NYL, combine, 0)

    def hand_back(x, c):
        for o in range(2):
            for zt in range(2):
                out_ref[o, x, :, zt * 128:zt * 128 + 128] = v[o, pl.ds(zt * 32 + x, 8, stride=64), :]
        return c

    lax.fori_loop(0, NXL, hand_back, 0)


def solution(mesh):
    sizes = tuple(mesh.shape[name] for name in ("gx", "gy", "band"))
    n_gx, n_gy, n_band = sizes

    def per_device(orbitals, potential, order):
        sem = pltpu.SemaphoreType.DMA
        return pl.pallas_call(
            functools.partial(kernel, sizes),
            out_shape=jax.ShapeDtypeStruct(orbitals.shape, F32),
            in_specs=[pl.BlockSpec(memory_space=pltpu.VMEM), pl.BlockSpec(memory_space=pltpu.VMEM),
                      pl.BlockSpec(memory_space=pltpu.SMEM)],
            out_specs=pl.BlockSpec(memory_space=pltpu.VMEM),
            scratch_shapes=[
                pltpu.VMEM((2, 2, YROWS, 2, XROWS, 128), F32),
                pltpu.VMEM((2, n_band, NYL, 2, NXL, 128), F32),
                pltpu.VMEM((NYL, 2, NXL, 128), F32),
                pltpu.VMEM((2, NYL * 2 * NXL, 128), F32),
                pltpu.VMEM((NYL * 2 * NXL, 128), F32),
                pltpu.VMEM((8, 128), F32), pltpu.VMEM((8, 128), F32), pltpu.VMEM((8, 128), F32),
                pltpu.VMEM((n_band - 1, 8, 128), F32), pltpu.VMEM((n_gy - 1, 8, 128), F32),
                pltpu.VMEM((n_gx - 1, 8, 128), F32),
                sem((2, 2, 4)), sem((2, 2, 4)),
                sem((2,)), sem((2,)), sem((2,)), sem((2,)), sem((3,)), sem((3,)),
            ],
            compiler_params=pltpu.CompilerParams(
                collective_id=0, has_side_effects=True, vmem_limit_bytes=32 * 1024 * 1024),
        )(orbitals, potential, order)

    return jax.shard_map(
        per_device, mesh=mesh,
        in_specs=(P("band", "gx", "gy", None), P("gx", "gy", None), P()),
        out_specs=P("band", "gx", "gy", None), check_vma=False,
    )
```

```python
import functools

import jax
import jax.numpy as jnp
from jax import lax
from jax.experimental import pallas as pl
from jax.experimental.pallas import tpu as pltpu
from jax.sharding import PartitionSpec as P

DEGREE = 8
MESH = pl.DeviceIdType.MESH
F32 = jnp.float32
FAR = 2.0 / (24.0 * 4.25)

NXL, NYL = 32, 8
X0, XROWS, Y0, YROWS = 8, 48, 4, 16


def kernel(sizes, orb_ref, pot_ref, order_ref, out_ref, a0, a1, b0, b1, g, pp, v, w, s1, s2, s3, r1, r2, r3,
           hs, hr, ps, pr, as_, ar, bs, br, rs, rr):
    n_gx, n_gy, n_band = sizes
    gx, gy, band = lax.axis_index("gx"), lax.axis_index("gy"), lax.axis_index("band")
    names = (("band", band, n_band), ("gy", gy, n_gy), ("gx", gx, n_gx))

    def clear(ref, *index):
        view = ref.at[index]
        view[...] = jnp.zeros(view.shape, F32)

    for ref in (a0, a1, b0, b1):
        for o in range(2):
            @pl.when(gy == 0)
            def _(ref=ref, o=o):
                clear(ref, o, slice(0, 4))

            @pl.when(gy == n_gy - 1)
            def _(ref=ref, o=o):
                clear(ref, o, slice(12, 16))

            @pl.when(gx == 0)
            def _(ref=ref, o=o):
                clear(ref, o, slice(2, 14), slice(None), slice(0, 8))

            @pl.when(gx == n_gx - 1)
            def _(ref=ref, o=o):
                clear(ref, o, slice(2, 14), slice(None), slice(40, 48))

    barrier = pltpu.get_barrier_semaphore()
    for name, me, count in names:
        def greet(d, c, name=name, me=me, count=count):
            pl.semaphore_signal(barrier, inc=1, device_id={name: lax.rem(me + d, count)}, device_id_type=MESH)
            return c
        lax.fori_loop(1, count, greet, 0)
    corners = [(gx > 0, gy > 0, -1, -1), (gx > 0, gy < n_gy - 1, -1, 1),
               (gx < n_gx - 1, gy > 0, 1, -1), (gx < n_gx - 1, gy < n_gy - 1, 1, 1)]
    diagonal = [jnp.logical_and(cx, cy) for cx, cy, _, _ in corners]
    met = n_band + n_gy + n_gx - 3
    for ok, (_, _, dx, dy) in zip(diagonal, corners):
        @pl.when(ok)
        def _(dx=dx, dy=dy):
            pl.semaphore_signal(barrier, inc=1, device_id={"gx": gx + dx, "gy": gy + dy}, device_id_type=MESH)
        met = met + ok.astype(jnp.int32)

    def bring(x, c):
        for zt in range(2):
            for o in range(2):
                v[o, pl.ds(zt * NXL + x, NYL, stride=2 * NXL), :] = orb_ref[o, x, :, zt * 128:zt * 128 + 128]
            w[pl.ds(zt * NXL + x, NYL, stride=2 * NXL), :] = pot_ref[x, :, zt * 128:zt * 128 + 128]
        return c

    lax.fori_loop(0, NXL, bring, 0)

    def place(y, c):
        for zt in range(2):
            for xt in range(4):
                rows_in = pl.ds(y * 64 + zt * NXL + 8 * xt, 8)
                for o in range(2):
                    a0[o, Y0 + y, zt, pl.ds(X0 + 8 * xt, 8), :] = v[o, rows_in, :]
                pp[y + 2, zt, pl.ds(X0 + 8 * xt, 8), :] = (w[rows_in, :] - 0.5) * (2.0 / 4.25)
        return c

    lax.fori_loop(0, NYL, place, 0)
    pl.semaphore_wait(barrier, met)

    low_x, high_x, low_y, high_y = gx > 0, gx < n_gx - 1, gy > 0, gy < n_gy - 1
    sends_ok = [low_y, high_y, low_x, high_x] + diagonal
    recvs_ok = [high_y, low_y, high_x, low_x] + diagonal[::-1]
    ids = [{"gy": gy - 1}, {"gy": gy + 1}, {"gx": gx - 1}, {"gx": gx + 1}] + [
        {"gx": gx + dx, "gy": gy + dy} for _, _, dx, dy in corners]
    xs, ys = pl.ds(X0, NXL), pl.ds(Y0, NYL)
    spans = [
        ((pl.ds(4, 4), xs), (pl.ds(12, 4), xs)),
        ((pl.ds(8, 4), xs), (pl.ds(0, 4), xs)),
        ((ys, pl.ds(8, 4)), (ys, pl.ds(40, 4))),
        ((ys, pl.ds(36, 4)), (ys, pl.ds(4, 4))),
        ((pl.ds(4, 2), pl.ds(8, 2)), (pl.ds(12, 2), pl.ds(40, 2))),
        ((pl.ds(10, 2), pl.ds(8, 2)), (pl.ds(2, 2), pl.ds(40, 2))),
        ((pl.ds(4, 2), pl.ds(38, 2)), (pl.ds(12, 2), pl.ds(6, 2))),
        ((pl.ds(10, 2), pl.ds(38, 2)), (pl.ds(2, 2), pl.ds(6, 2))),
    ]
    yp = pl.ds(2, NYL)
    pot_spans = [
        ((pl.ds(2, 2), xs), (pl.ds(10, 2), xs)),
        ((pl.ds(8, 2), xs), (pl.ds(0, 2), xs)),
        ((yp, pl.ds(8, 2)), (yp, pl.ds(40, 2))),
        ((yp, pl.ds(38, 2)), (yp, pl.ds(6, 2))),
    ]

    even, odd = (a0, a1), (b0, b1)

    def halo(o, p, way):
        (sy, sx), (dy, dx) = spans[way]
        return pltpu.make_async_remote_copy(
            src_ref=even[p].at[o, sy, :, sx, :], dst_ref=even[p].at[o, dy, :, dx, :],
            send_sem=hs.at[o, p, way], recv_sem=hr.at[o, p, way],
            device_id=ids[way], device_id_type=MESH)

    def pot_halo(way):
        (sy, sx), (dy, dx) = pot_spans[way]
        return pltpu.make_async_remote_copy(
            src_ref=pp.at[sy, :, sx, :], dst_ref=pp.at[dy, :, dx, :],
            send_sem=ps.at[way], recv_sem=pr.at[way], device_id=ids[way], device_id_type=MESH)

    def send(ways, copy):
        for way in ways:
            @pl.when(sends_ok[way])
            def _(way=way):
                copy(way).start()

    def arrive(ways, copy):
        for way in ways:
            @pl.when(recvs_ok[way])
            def _(way=way):
                copy(way).wait_recv()

            @pl.when(sends_ok[way])
            def _(way=way):
                copy(way).wait_send()

    lane = lax.broadcasted_iota(jnp.int32, (8, 128), 1)
    sub = lax.broadcasted_iota(jnp.int32, (8, 128), 0)

    def cells(cur, prev, yy, r):
        mid = [cur[yy, zt, pl.ds(r, 8), :] for zt in range(2)]
        none = jnp.zeros_like(mid[0])
        values = []
        for zt in range(2):
            m = mid[zt]
            after = mid[1] if zt == 0 else none
            before = mid[0] if zt == 1 else none
            near = cur[yy, zt, pl.ds(r - 1, 8), :] + cur[yy, zt, pl.ds(r + 1, 8), :]
            near = near + (cur[yy - 1, zt, pl.ds(r, 8), :] + cur[yy + 1, zt, pl.ds(r, 8), :])
            near = near + (pltpu.roll(jnp.where(lane < 1, after, m), 127, 1)
                           + pltpu.roll(jnp.where(lane >= 127, before, m), 1, 1))
            far = cur[yy, zt, pl.ds(r - 2, 8), :] + cur[yy, zt, pl.ds(r + 2, 8), :]
            far = far + (cur[yy - 2, zt, pl.ds(r, 8), :] + cur[yy + 2, zt, pl.ds(r, 8), :])
            far = far + (pltpu.roll(jnp.where(lane < 2, after, m), 126, 1)
                         + pltpu.roll(jnp.where(lane >= 126, before, m), 2, 1))
            value = pp[yy - 2, zt, pl.ds(r, 8), :] * m + (far - 16.0 * near) * FAR
            values.append(value * 0.5 if prev is None else value - prev[yy, zt, pl.ds(r, 8), :])
        return values

    ALIGNED = (8, 16, 24, 32)
    SHIFTED = (6, 14, 22, 30, 38)

    def odd_step(o, j):
        p = j % 2
        cur, prev, new = even[p].at[o], None if j == 0 else odd[1 - p].at[o], odd[p].at[o]

        def put(y, offsets):
            for r in offsets:
                for zt, value in enumerate(cells(cur, prev, y, r)):
                    new[y, zt, pl.ds(r, 8), :] = value

        for y in range(4, 12):
            put(y, SHIFTED)
        for ok, y in ((low_y, 2), (high_y, 12)):
            @pl.when(ok)
            def _(y=y):
                put(y, ALIGNED)
                put(y + 1, ALIGNED)

        @pl.when(gx == 0)
        def _():
            new[4:12, :, 6:8, :] = jnp.zeros((8, 2, 2, 128), F32)

        @pl.when(gx == n_gx - 1)
        def _():
            new[4:12, :, 40:42, :] = jnp.zeros((8, 2, 2, 128), F32)

    def even_step(o, j):
        p = j % 2
        cur, prev, new = odd[p].at[o], even[p].at[o], even[1 - p].at[o]
        last = j == DEGREE // 2 - 1

        def half(i):
            for y in range(4 + 4 * i, 8 + 4 * i):
                for r in ALIGNED:
                    for zt, value in enumerate(cells(cur, prev, y, r)):
                        if last:
                            g[o, band, y - 4, zt, pl.ds(r - X0, 8), :] = value
                        else:
                            new[y, zt, pl.ds(r, 8), :] = value

        half(0)
        if not last:
            send((0,), functools.partial(halo, o, 1 - p))
        half(1)
        if not last:
            send((1, 2, 3, 4, 5, 6, 7), functools.partial(halo, o, 1 - p))

    def quarter(o, d, turn):
        peer = lax.rem(band + d, n_band)
        part = lax.rem(peer + turn, n_band)
        block = g.at[o, band, pl.ds(2 * part, 2)]
        sem = (as_.at[o], ar.at[o]) if turn == 0 else (bs.at[o], br.at[o])
        return pltpu.make_async_remote_copy(
            src_ref=block, dst_ref=block, send_sem=sem[0], recv_sem=sem[1],
            device_id={"band": peer}, device_id_type=MESH)

    for o in range(2):
        send(range(8), functools.partial(halo, o, 0))
        if o == 0:
            send(range(4), pot_halo)

    for j in range(DEGREE // 2):
        def block(o, c, j=j):
            arrive(range(8), functools.partial(halo, o, j % 2))
            if j == 0:
                @pl.when(o == 0)
                def _():
                    arrive(range(4), pot_halo)
            odd_step(o, j)
            even_step(o, j)
            if j == DEGREE // 2 - 1:
                for d in range(1, n_band):
                    quarter(o, d, 0).start()
            return c

        lax.fori_loop(0, 2, block, 0)

    def both(o, first, count, sems):
        block = g.at[o, pl.ds(0, first), pl.ds(0, count)]
        pltpu.make_async_copy(block, block, sems[1].at[o]).wait()
        pltpu.make_async_copy(block, block, sems[0].at[o]).wait()

    for o in range(2):
        both(o, n_band - 1, 2, (as_, ar))

    orbs = 2 * n_band
    pairs = [(i, j) for i in range(orbs) for j in range(i + 1)]

    def correlate(t, sums):
        y, zt = 2 * band + t // 2, t % 2
        sums = list(sums)
        for xt in range(4):
            f = [g[i % 2, i // 2, y, zt, pl.ds(8 * xt, 8), :] for i in range(orbs)]
            sums = [a + f[i] * f[j] for a, (i, j) in zip(sums, pairs)]
        return tuple(sums)

    sums = lax.fori_loop(0, 4, correlate, tuple(jnp.zeros((8, 128), F32) for _ in pairs))
    flat = {}
    for a, (i, j) in zip(sums, pairs):
        flat[i, j] = flat[j, i] = jnp.sum(a, axis=0, keepdims=True)
    corr = jnp.zeros((8, 128), F32)
    for j in range(orbs):
        column = jnp.sum(jnp.concatenate([flat[i, j] for i in range(orbs)], axis=0), axis=1, keepdims=True)
        corr = jnp.where(lane == j, column, corr)

    for index, ((name, me, count), src, dst) in enumerate(zip(names, (s1, s2, s3), (r1, r2, r3))):
        src[...] = corr

        def give(d, c, name=name, me=me, count=count, src=src, dst=dst, index=index):
            pltpu.make_async_remote_copy(
                src_ref=src, dst_ref=dst.at[d - 1], send_sem=rs.at[index], recv_sem=rr.at[index],
                device_id={name: lax.rem(me + d, count)}, device_id_type=MESH).start()
            return c

        lax.fori_loop(1, count, give, 0)
        if index == 0:
            for turn in range(1, n_band):
                for o in range(2):
                    for d in range(1, n_band):
                        quarter(o, d, turn).start()
        pltpu.make_async_copy(dst, dst, rr.at[index]).wait()
        for d in range(count - 1):
            corr = corr + dst[d]
    total_cells = float(n_gx * NXL * n_gy * NYL * 256)
    state = jnp.where(lane < 8, corr * (1.0 / total_cells), jnp.where(lane == sub + 8, 1.0, 0.0))
    waiting = jnp.ones((8, 128), F32)
    pivots = jnp.ones((8, 128), F32)
    for position in range(orbs):
        j = order_ref[position]
        row = jnp.sum(jnp.where(sub == j, state, 0.0), axis=0, keepdims=True)
        column = jnp.sum(jnp.where(lane == j, state, 0.0), axis=1, keepdims=True)
        pivot = jnp.sum(jnp.where(lane[0:1] == j, row, 0.0), axis=1, keepdims=True)
        waiting = jnp.where(sub == j, 0.0, waiting)
        state = state - (waiting * (column / pivot)) * row
        pivots = jnp.where(sub == j, pivot, pivots)
    mixing = state / jnp.sqrt(pivots)

    weights = []
    for o in range(2):
        own = jnp.sum(jnp.where(sub == 2 * band + o, mixing, 0.0), axis=0, keepdims=True)
        weights.append([jnp.broadcast_to(jnp.sum(jnp.where(lane[0:1] == 8 + j, own, 0.0), axis=1, keepdims=True), (8, 128))
                        for j in range(orbs)])

    for o in range(2):
        both(o, n_band - 1, 6, (bs, br))
    for index, dst in enumerate((r1, r2, r3)):
        pltpu.make_async_copy(dst, dst, rs.at[index]).wait()

    def combine(y, c):
        for zt in range(2):
            for xt in range(4):
                f = [g[i % 2, i // 2, y, zt, pl.ds(8 * xt, 8), :] for i in range(orbs)]
                for o in range(2):
                    total = weights[o][0] * f[0]
                    for i in range(1, orbs):
                        total = total + weights[o][i] * f[i]
                    v[o, pl.ds(y * 64 + zt * 32 + 8 * xt, 8), :] = total
        return c

    lax.fori_loop(0, NYL, combine, 0)

    def hand_back(x, c):
        for o in range(2):
            for zt in range(2):
                out_ref[o, x, :, zt * 128:zt * 128 + 128] = v[o, pl.ds(zt * 32 + x, 8, stride=64), :]
        return c

    lax.fori_loop(0, NXL, hand_back, 0)


def solution(mesh):
    sizes = tuple(mesh.shape[name] for name in ("gx", "gy", "band"))
    n_gx, n_gy, n_band = sizes

    def per_device(orbitals, potential, order):
        sem = pltpu.SemaphoreType.DMA
        return pl.pallas_call(
            functools.partial(kernel, sizes),
            out_shape=jax.ShapeDtypeStruct(orbitals.shape, F32),
            in_specs=[pl.BlockSpec(memory_space=pltpu.VMEM), pl.BlockSpec(memory_space=pltpu.VMEM),
                      pl.BlockSpec(memory_space=pltpu.SMEM)],
            out_specs=pl.BlockSpec(memory_space=pltpu.VMEM),
            scratch_shapes=[
                *[pltpu.VMEM((2, YROWS, 2, XROWS, 128), F32)] * 4,
                pltpu.VMEM((2, n_band, NYL, 2, NXL, 128), F32),
                pltpu.VMEM((NYL + 4, 2, XROWS, 128), F32),
                pltpu.VMEM((2, NYL * 2 * NXL, 128), F32),
                pltpu.VMEM((NYL * 2 * NXL, 128), F32),
                pltpu.VMEM((8, 128), F32), pltpu.VMEM((8, 128), F32), pltpu.VMEM((8, 128), F32),
                pltpu.VMEM((n_band - 1, 8, 128), F32), pltpu.VMEM((n_gy - 1, 8, 128), F32),
                pltpu.VMEM((n_gx - 1, 8, 128), F32),
                sem((2, 2, 8)), sem((2, 2, 8)), sem((4,)), sem((4,)),
                sem((2,)), sem((2,)), sem((2,)), sem((2,)), sem((3,)), sem((3,)),
            ],
            compiler_params=pltpu.CompilerParams(
                collective_id=0, has_side_effects=True, vmem_limit_bytes=32 * 1024 * 1024),
        )(orbitals, potential, order)

    return jax.shard_map(
        per_device, mesh=mesh,
        in_specs=(P("band", "gx", "gy", None), P("gx", "gy", None), P()),
        out_specs=P("band", "gx", "gy", None), check_vma=False,
    )
```

```python
import functools

import jax
import jax.numpy as jnp
from jax import lax
from jax.experimental import pallas as pl
from jax.experimental.pallas import tpu as pltpu
from jax.sharding import PartitionSpec as P

DEGREE = 8
MESH = pl.DeviceIdType.MESH
F32 = jnp.float32
FAR = 2.0 / (24.0 * 4.25)

NXL, NYL = 32, 8
X0, XROWS, Y0, YROWS = 8, 48, 4, 16


def kernel(sizes, orb_ref, pot_ref, order_ref, out_ref, a0, a1, b0, b1, g, pp, v, w, s1, s2, s3, r1, r2, r3,
           hs, hr, ps, pr, as_, ar, bs, br, fr, rs, rr):
    n_gx, n_gy, n_band = sizes
    gx, gy, band = lax.axis_index("gx"), lax.axis_index("gy"), lax.axis_index("band")
    names = (("band", band, n_band), ("gy", gy, n_gy), ("gx", gx, n_gx))

    def clear(ref, *index):
        view = ref.at[index]
        view[...] = jnp.zeros(view.shape, F32)

    for ref in (a0, a1, b0, b1):
        for o in range(2):
            @pl.when(gy == 0)
            def _(ref=ref, o=o):
                clear(ref, o, slice(0, 4))

            @pl.when(gy == n_gy - 1)
            def _(ref=ref, o=o):
                clear(ref, o, slice(12, 16))

            @pl.when(gx == 0)
            def _(ref=ref, o=o):
                clear(ref, o, slice(2, 14), slice(None), slice(0, 8))

            @pl.when(gx == n_gx - 1)
            def _(ref=ref, o=o):
                clear(ref, o, slice(2, 14), slice(None), slice(40, 48))

    barrier = pltpu.get_barrier_semaphore()
    for name, me, count in names:
        def greet(d, c, name=name, me=me, count=count):
            pl.semaphore_signal(barrier, inc=1, device_id={name: lax.rem(me + d, count)}, device_id_type=MESH)
            return c
        lax.fori_loop(1, count, greet, 0)
    corners = [(gx > 0, gy > 0, -1, -1), (gx > 0, gy < n_gy - 1, -1, 1),
               (gx < n_gx - 1, gy > 0, 1, -1), (gx < n_gx - 1, gy < n_gy - 1, 1, 1)]
    diagonal = [jnp.logical_and(cx, cy) for cx, cy, _, _ in corners]
    met = n_band + n_gy + n_gx - 3
    for ok, (_, _, dx, dy) in zip(diagonal, corners):
        @pl.when(ok)
        def _(dx=dx, dy=dy):
            pl.semaphore_signal(barrier, inc=1, device_id={"gx": gx + dx, "gy": gy + dy}, device_id_type=MESH)
        met = met + ok.astype(jnp.int32)

    def bring(x, c):
        for zt in range(2):
            for o in range(2):
                v[o, pl.ds(zt * NXL + x, NYL, stride=2 * NXL), :] = orb_ref[o, x, :, zt * 128:zt * 128 + 128]
            w[pl.ds(zt * NXL + x, NYL, stride=2 * NXL), :] = pot_ref[x, :, zt * 128:zt * 128 + 128]
        return c

    lax.fori_loop(0, NXL, bring, 0)

    def place(y, c):
        for zt in range(2):
            for xt in range(4):
                rows_in = pl.ds(y * 64 + zt * NXL + 8 * xt, 8)
                for o in range(2):
                    a0[o, Y0 + y, zt, pl.ds(X0 + 8 * xt, 8), :] = v[o, rows_in, :]
                pp[y + 2, zt, pl.ds(X0 + 8 * xt, 8), :] = (w[rows_in, :] - 0.5) * (2.0 / 4.25)
        return c

    lax.fori_loop(0, NYL, place, 0)
    pl.semaphore_wait(barrier, met)

    low_x, high_x, low_y, high_y = gx > 0, gx < n_gx - 1, gy > 0, gy < n_gy - 1
    sends_ok = [low_y, high_y, low_x, high_x] + diagonal
    recvs_ok = [high_y, low_y, high_x, low_x] + diagonal[::-1]
    ids = [{"gy": gy - 1}, {"gy": gy + 1}, {"gx": gx - 1}, {"gx": gx + 1}] + [
        {"gx": gx + dx, "gy": gy + dy} for _, _, dx, dy in corners]
    xs, ys = pl.ds(X0, NXL), pl.ds(Y0, NYL)
    spans = [
        ((pl.ds(4, 4), xs), (pl.ds(12, 4), xs)),
        ((pl.ds(8, 4), xs), (pl.ds(0, 4), xs)),
        ((ys, pl.ds(8, 4)), (ys, pl.ds(40, 4))),
        ((ys, pl.ds(36, 4)), (ys, pl.ds(4, 4))),
        ((pl.ds(4, 2), pl.ds(8, 2)), (pl.ds(12, 2), pl.ds(40, 2))),
        ((pl.ds(10, 2), pl.ds(8, 2)), (pl.ds(2, 2), pl.ds(40, 2))),
        ((pl.ds(4, 2), pl.ds(38, 2)), (pl.ds(12, 2), pl.ds(6, 2))),
        ((pl.ds(10, 2), pl.ds(38, 2)), (pl.ds(2, 2), pl.ds(6, 2))),
    ]
    yp = pl.ds(2, NYL)
    pot_spans = [
        ((pl.ds(2, 2), xs), (pl.ds(10, 2), xs)),
        ((pl.ds(8, 2), xs), (pl.ds(0, 2), xs)),
        ((yp, pl.ds(8, 2)), (yp, pl.ds(40, 2))),
        ((yp, pl.ds(38, 2)), (yp, pl.ds(6, 2))),
    ]

    even, odd = (a0, a1), (b0, b1)

    def halo(o, p, way):
        (sy, sx), (dy, dx) = spans[way]
        return pltpu.make_async_remote_copy(
            src_ref=even[p].at[o, sy, :, sx, :], dst_ref=even[p].at[o, dy, :, dx, :],
            send_sem=hs.at[o, p, way], recv_sem=hr.at[o, p, way],
            device_id=ids[way], device_id_type=MESH)

    def pot_halo(way):
        (sy, sx), (dy, dx) = pot_spans[way]
        return pltpu.make_async_remote_copy(
            src_ref=pp.at[sy, :, sx, :], dst_ref=pp.at[dy, :, dx, :],
            send_sem=ps.at[way], recv_sem=pr.at[way], device_id=ids[way], device_id_type=MESH)

    def send(ways, copy):
        for way in ways:
            @pl.when(sends_ok[way])
            def _(way=way):
                copy(way).start()

    def arrive(ways, copy):
        for way in ways:
            @pl.when(recvs_ok[way])
            def _(way=way):
                copy(way).wait_recv()

            @pl.when(sends_ok[way])
            def _(way=way):
                copy(way).wait_send()

    lane = lax.broadcasted_iota(jnp.int32, (8, 128), 1)
    sub = lax.broadcasted_iota(jnp.int32, (8, 128), 0)

    def cells(cur, prev, yy, r):
        mid = [cur[yy, zt, pl.ds(r, 8), :] for zt in range(2)]
        none = jnp.zeros_like(mid[0])
        values = []
        for zt in range(2):
            m = mid[zt]
            after = mid[1] if zt == 0 else none
            before = mid[0] if zt == 1 else none
            near = cur[yy, zt, pl.ds(r - 1, 8), :] + cur[yy, zt, pl.ds(r + 1, 8), :]
            near = near + (cur[yy - 1, zt, pl.ds(r, 8), :] + cur[yy + 1, zt, pl.ds(r, 8), :])
            near = near + (pltpu.roll(jnp.where(lane < 1, after, m), 127, 1)
                           + pltpu.roll(jnp.where(lane >= 127, before, m), 1, 1))
            far = cur[yy, zt, pl.ds(r - 2, 8), :] + cur[yy, zt, pl.ds(r + 2, 8), :]
            far = far + (cur[yy - 2, zt, pl.ds(r, 8), :] + cur[yy + 2, zt, pl.ds(r, 8), :])
            far = far + (pltpu.roll(jnp.where(lane < 2, after, m), 126, 1)
                         + pltpu.roll(jnp.where(lane >= 126, before, m), 2, 1))
            value = pp[yy - 2, zt, pl.ds(r, 8), :] * m + (far - 16.0 * near) * FAR
            values.append(value * 0.5 if prev is None else value - prev[yy, zt, pl.ds(r, 8), :])
        return values

    ALIGNED = (8, 16, 24, 32)
    SHIFTED = (6, 14, 22, 30, 38)

    def odd_step(o, j):
        p = j % 2
        cur, prev, new = even[p].at[o], None if j == 0 else odd[1 - p].at[o], odd[p].at[o]

        def put(y, offsets):
            for r in offsets:
                for zt, value in enumerate(cells(cur, prev, y, r)):
                    new[y, zt, pl.ds(r, 8), :] = value

        for y in range(4, 12):
            put(y, SHIFTED)
        for ok, y in ((low_y, 2), (high_y, 12)):
            @pl.when(ok)
            def _(y=y):
                put(y, ALIGNED)
                put(y + 1, ALIGNED)

        @pl.when(gx == 0)
        def _():
            new[4:12, :, 6:8, :] = jnp.zeros((8, 2, 2, 128), F32)

        @pl.when(gx == n_gx - 1)
        def _():
            new[4:12, :, 40:42, :] = jnp.zeros((8, 2, 2, 128), F32)

    def even_step(o, j):
        p = j % 2
        cur, prev, new = odd[p].at[o], even[p].at[o], even[1 - p].at[o]
        last = j == DEGREE // 2 - 1

        def half(i):
            for y in range(4 + 4 * i, 8 + 4 * i):
                for r in ALIGNED:
                    for zt, value in enumerate(cells(cur, prev, y, r)):
                        if last:
                            g[o, band, y - 4, zt, pl.ds(r - X0, 8), :] = value
                        else:
                            new[y, zt, pl.ds(r, 8), :] = value

        half(0)
        if not last:
            send((0,), functools.partial(halo, o, 1 - p))
        half(1)
        if not last:
            send((1, 2, 3, 4, 5, 6, 7), functools.partial(halo, o, 1 - p))

    def piece(o, source, part, peer, sends, recvs):
        block = g.at[o, source, pl.ds(2 * part, 2)]
        return pltpu.make_async_remote_copy(
            src_ref=block, dst_ref=block, send_sem=sends, recv_sem=recvs,
            device_id={"band": peer}, device_id_type=MESH)

    def around(step):
        return lax.rem(band + step + n_band, n_band)

    right, left, across = around(1), around(-1), around(2)

    def quarter(o, peer):
        return piece(o, band, peer, peer, as_.at[o], ar.at[o])

    def own_ahead():
        for part in (left, band):
            piece(0, band, part, right, bs.at[0], fr.at[0]).start()
        for part in (band, right):
            piece(1, band, part, left, bs.at[1], fr.at[1]).start()

    def own_rest():
        piece(0, band, across, right, bs.at[0], br.at[0]).start()
        piece(1, band, across, left, bs.at[1], br.at[1]).start()
        for part in (band, right, across):
            piece(0, band, part, left, bs.at[0], br.at[0]).start()
        for part in (band, left, across):
            piece(1, band, part, right, bs.at[1], br.at[1]).start()

    def pass_on(parts_right, parts_left):
        for part in parts_right:
            piece(0, left, part, right, bs.at[0], br.at[0]).start()
        for part in parts_left:
            piece(1, right, part, left, bs.at[1], br.at[1]).start()

    def passed_in():
        for o in range(2):
            block = g.at[o, 0, pl.ds(0, 4)]
            pltpu.make_async_copy(block, block, fr.at[o]).wait()

    for o in range(2):
        send(range(8), functools.partial(halo, o, 0))
        if o == 0:
            send(range(4), pot_halo)

    for j in range(DEGREE // 2):
        def block(o, c, j=j):
            arrive(range(8), functools.partial(halo, o, j % 2))
            if j == 0:
                @pl.when(o == 0)
                def _():
                    arrive(range(4), pot_halo)
            odd_step(o, j)
            even_step(o, j)
            if j == DEGREE // 2 - 1:
                for peer in (right, left, across):
                    quarter(o, peer).start()
            return c

        lax.fori_loop(0, 2, block, 0)

    def both(o, first, count, sems):
        block = g.at[o, pl.ds(0, first), pl.ds(0, count)]
        pltpu.make_async_copy(block, block, sems[1].at[o]).wait()
        pltpu.make_async_copy(block, block, sems[0].at[o]).wait()

    for o in range(2):
        both(o, n_band - 1, 2, (as_, ar))

    orbs = 2 * n_band
    pairs = [(i, j) for i in range(orbs) for j in range(i + 1)]

    def correlate(t, sums):
        y, zt = 2 * band + t // 2, t % 2
        sums = list(sums)
        for xt in range(4):
            f = [g[i % 2, i // 2, y, zt, pl.ds(8 * xt, 8), :] for i in range(orbs)]
            sums = [a + f[i] * f[j] for a, (i, j) in zip(sums, pairs)]
        return tuple(sums)

    sums = lax.fori_loop(0, 4, correlate, tuple(jnp.zeros((8, 128), F32) for _ in pairs))
    flat = {}
    for a, (i, j) in zip(sums, pairs):
        flat[i, j] = flat[j, i] = jnp.sum(a, axis=0, keepdims=True)
    corr = jnp.zeros((8, 128), F32)
    for j in range(orbs):
        column = jnp.sum(jnp.concatenate([flat[i, j] for i in range(orbs)], axis=0), axis=1, keepdims=True)
        corr = jnp.where(lane == j, column, corr)

    for index, ((name, me, count), src, dst) in enumerate(zip(names, (s1, s2, s3), (r1, r2, r3))):
        src[...] = corr

        def give(d, c, name=name, me=me, count=count, src=src, dst=dst, index=index):
            pltpu.make_async_remote_copy(
                src_ref=src, dst_ref=dst.at[d - 1], send_sem=rs.at[index], recv_sem=rr.at[index],
                device_id={name: lax.rem(me + d, count)}, device_id_type=MESH).start()
            return c

        lax.fori_loop(1, count, give, 0)
        if index == 0:
            own_ahead()
            pass_on((band,), (band,))
            own_rest()
        if index == 1:
            passed_in()
            pass_on((left, across), (right, across))
        pltpu.make_async_copy(dst, dst, rr.at[index]).wait()
        for d in range(count - 1):
            corr = corr + dst[d]
    total_cells = float(n_gx * NXL * n_gy * NYL * 256)
    state = jnp.where(lane < 8, corr * (1.0 / total_cells), jnp.where(lane == sub + 8, 1.0, 0.0))
    waiting = jnp.ones((8, 128), F32)
    pivots = jnp.ones((8, 128), F32)
    for position in range(orbs):
        j = order_ref[position]
        row = jnp.sum(jnp.where(sub == j, state, 0.0), axis=0, keepdims=True)
        column = jnp.sum(jnp.where(lane == j, state, 0.0), axis=1, keepdims=True)
        pivot = jnp.sum(jnp.where(lane[0:1] == j, row, 0.0), axis=1, keepdims=True)
        waiting = jnp.where(sub == j, 0.0, waiting)
        state = state - (waiting * (column / pivot)) * row
        pivots = jnp.where(sub == j, pivot, pivots)
    mixing = state / jnp.sqrt(pivots)

    weights = []
    for o in range(2):
        own = jnp.sum(jnp.where(sub == 2 * band + o, mixing, 0.0), axis=0, keepdims=True)
        weights.append([jnp.broadcast_to(jnp.sum(jnp.where(lane[0:1] == 8 + j, own, 0.0), axis=1, keepdims=True), (8, 128))
                        for j in range(orbs)])

    for o in range(2):
        seven = a0.at[o, pl.ds(0, 14), :, pl.ds(0, NXL)]
        nine = g.at[o, pl.ds(0, 3), pl.ds(0, 6)]
        pltpu.make_async_copy(seven, seven, br.at[o]).wait()
        pltpu.make_async_copy(nine, nine, bs.at[o]).wait()
    for index, dst in enumerate((r1, r2, r3)):
        pltpu.make_async_copy(dst, dst, rs.at[index]).wait()

    def combine(y, c):
        for zt in range(2):
            for xt in range(4):
                f = [g[i % 2, i // 2, y, zt, pl.ds(8 * xt, 8), :] for i in range(orbs)]
                for o in range(2):
                    total = weights[o][0] * f[0]
                    for i in range(1, orbs):
                        total = total + weights[o][i] * f[i]
                    v[o, pl.ds(y * 64 + zt * 32 + 8 * xt, 8), :] = total
        return c

    lax.fori_loop(0, NYL, combine, 0)

    def hand_back(x, c):
        for o in range(2):
            for zt in range(2):
                out_ref[o, x, :, zt * 128:zt * 128 + 128] = v[o, pl.ds(zt * 32 + x, 8, stride=64), :]
        return c

    lax.fori_loop(0, NXL, hand_back, 0)


def solution(mesh):
    sizes = tuple(mesh.shape[name] for name in ("gx", "gy", "band"))
    n_gx, n_gy, n_band = sizes

    def per_device(orbitals, potential, order):
        sem = pltpu.SemaphoreType.DMA
        return pl.pallas_call(
            functools.partial(kernel, sizes),
            out_shape=jax.ShapeDtypeStruct(orbitals.shape, F32),
            in_specs=[pl.BlockSpec(memory_space=pltpu.VMEM), pl.BlockSpec(memory_space=pltpu.VMEM),
                      pl.BlockSpec(memory_space=pltpu.SMEM)],
            out_specs=pl.BlockSpec(memory_space=pltpu.VMEM),
            scratch_shapes=[
                *[pltpu.VMEM((2, YROWS, 2, XROWS, 128), F32)] * 4,
                pltpu.VMEM((2, n_band, NYL, 2, NXL, 128), F32),
                pltpu.VMEM((NYL + 4, 2, XROWS, 128), F32),
                pltpu.VMEM((2, NYL * 2 * NXL, 128), F32),
                pltpu.VMEM((NYL * 2 * NXL, 128), F32),
                pltpu.VMEM((8, 128), F32), pltpu.VMEM((8, 128), F32), pltpu.VMEM((8, 128), F32),
                pltpu.VMEM((n_band - 1, 8, 128), F32), pltpu.VMEM((n_gy - 1, 8, 128), F32),
                pltpu.VMEM((n_gx - 1, 8, 128), F32),
                sem((2, 2, 8)), sem((2, 2, 8)), sem((4,)), sem((4,)),
                sem((2,)), sem((2,)), sem((2,)), sem((2,)), sem((2,)), sem((3,)), sem((3,)),
            ],
            compiler_params=pltpu.CompilerParams(
                collective_id=0, has_side_effects=True, vmem_limit_bytes=32 * 1024 * 1024),
        )(orbitals, potential, order)

    return jax.shard_map(
        per_device, mesh=mesh,
        in_specs=(P("band", "gx", "gy", None), P("gx", "gy", None), P()),
        out_specs=P("band", "gx", "gy", None), check_vma=False,
    )
```
